32 devices in a mesh: seq: 8 (over y, x, core), head: 4 (over z).
Axes of the slice: x: 2, y: 2, z: 4, core: 2. Of those that a mesh axis runs over, the one named last changes fastest.
Arguments:
- queries: bfloat16 [8192, 1024], P(('seq', 'head')), may hold values from -200 to 200
- keys: bfloat16 [8192, 512], P(('seq', 'head')), may hold values from -6.5 to 6.5
- values: bfloat16 [8192, 512], P(('seq', 'head')), may hold values from -6 to 6
- visible: int32 [8, 4], P('seq'), may hold values 0 or 1
Outputs:
- attended: bfloat16 [8192, 1024], P(('seq', 'head'))
The draws below stay inside these ranges and needn't reach their ends.
All inputs are finite; a program needn't handle non-finite values. No bound on the sum of `visible` on one device may be relied on, other than what follows from the above.
Results may differ from the reference program's by a relative error of at most 0.0045.
Values may be sent and summed in bfloat16 or wider, within the bound.
No kernel may reach another device: no remote copies, remote signals or barrier semaphores. Data moves between devices by JAX's collectives and lax.ppermute only.
A program may use at most 128 MiB of HBM per device.

```python
import jax
import jax.numpy as jnp
from jax import lax

HEAD_SIZE = 128
QUERY_PER_KV = 2
KEY_VALUE_HEADS = 4
HQ = 8
SEQUENCE_TOKENS = 8192
N_SEQ = 8


def joint_draw(key):
    query_key = jax.random.fold_in(key, 11)
    key_random_seed = jax.random.fold_in(key, 12)
    query_vals = jnp.clip(jax.random.normal(query_key, (SEQUENCE_TOKENS, HQ * HEAD_SIZE), jnp.float32), -6.0, 6.0)
    key_samples = jnp.clip(jax.random.normal(key_random_seed, (SEQUENCE_TOKENS, KEY_VALUE_HEADS * HEAD_SIZE), jnp.float32), -6.0, 6.0)
    return (query_vals, key_samples)


def draw_queries(key, part):
    return joint_draw(key)[0].astype(jnp.bfloat16)


def draw_keys(key, part):
    return joint_draw(key)[1].astype(jnp.bfloat16)


def place_ends(array, rng, low, largest):
    dims = array.shape
    index_at = [jax.random.randint(jax.random.fold_in(rng, axis), (), 0, dims[axis]) for axis in range(len(dims))]
    array = array.at[tuple(index_at)].set(low)
    longest = dims.index(max(dims))
    index_at[longest] = (index_at[longest] + 1) % dims[longest]
    return array.at[tuple(index_at)].set(largest)


def block_scale(stream_key, extent, pieces, low, largest):
    def one(position, parts):
        steps = jax.random.uniform(jax.random.fold_in(jax.random.fold_in(stream_key, 6), position), (parts,), jnp.float32, low / len(pieces), largest / len(pieces))
        return jnp.repeat(jnp.exp(steps), extent[position] // parts).reshape((-1,) + (1,) * (len(extent) - position - 1))

    factor_of = one(*pieces[0])
    for cut in pieces[1:]:
        factor_of = factor_of * one(*cut)
    return factor_of


def gaussian(own_key, dims, scale, reach, shards=(), kind=jnp.bfloat16):
    array = scale * jax.random.normal(own_key, dims, jnp.float32)
    if shards:
        array = array * block_scale(own_key, dims, shards, -0.22, 0.18)
    return jnp.clip(array, -reach, reach).astype(kind)


def setup_inputs(seed: int = 0) -> dict:
    seeds = jax.random.split(jax.random.key(seed), 5)
    return {
        "queries": draw_queries(jax.random.fold_in(seeds[4], 71), 0),
        "keys": draw_keys(jax.random.fold_in(seeds[4], 71), 0),
        "values": gaussian(seeds[2], (SEQUENCE_TOKENS, KEY_VALUE_HEADS * HEAD_SIZE), 1.0, 6.0, ((0, 32),)),
        "visible": place_ends((jax.random.randint(seeds[3], (N_SEQ, 4), 0, 4) < 3).astype(jnp.int32), jax.random.fold_in(seeds[3], 1), 0, 1),
    }


attn_scale = 168.0 ** -0.5
powers = (1, 2, 4, 8)


def reference(queries, keys, values, visible):
    tokens_all = queries.shape[0]
    block_length = tokens_all // N_SEQ
    query_block_list = queries.reshape(N_SEQ, block_length, KEY_VALUE_HEADS, QUERY_PER_KV, HEAD_SIZE)
    key_block_list = keys.reshape(N_SEQ, block_length, KEY_VALUE_HEADS, HEAD_SIZE)
    value_block_list = values.reshape(N_SEQ, block_length, KEY_VALUE_HEADS, HEAD_SIZE)

    def one_block(index):
        index = index.astype(jnp.int32)
        own_query = lax.dynamic_index_in_dim(query_block_list, index, 0, keepdims=False)
        key_list = [lax.dynamic_index_in_dim(key_block_list, index, 0, keepdims=False)]
        value_list = [lax.dynamic_index_in_dim(value_block_list, index, 0, keepdims=False)]
        flags = []
        for slot, distance in enumerate(powers):
            source = jnp.maximum(index - distance, 0).astype(jnp.int32)
            key_list.append(lax.dynamic_index_in_dim(key_block_list, source, 0, keepdims=False))
            value_list.append(lax.dynamic_index_in_dim(value_block_list, source, 0, keepdims=False))
            flags.append((visible[index, slot] != 0) & (index >= distance))
        all_keys = jnp.concatenate(key_list, axis=0)
        all_values = jnp.concatenate(value_list, axis=0)
        scores = jnp.einsum("qhgd,khd->hgqk", own_query.astype(jnp.float32), all_keys.astype(jnp.float32)) * attn_scale
        row_index = jnp.arange(block_length)[:, None]
        column = jnp.arange(5 * block_length)[None, :]
        region = column // block_length
        flag_arr = jnp.stack(flags)
        remote_ok = jnp.any((region[None] == (jnp.arange(4) + 1)[:, None, None]) & flag_arr[:, None, None], axis=0)
        allowed = jnp.where(region == 0, column <= row_index, remote_ok)
        masked = jnp.where(allowed, scores, -1e30)
        peak = jnp.max(masked, axis=-1, keepdims=True)
        weights = jnp.where(allowed, jnp.exp(masked - peak), 0.0)
        total = jnp.sum(weights, axis=-1)
        rounded = lax.optimization_barrier(weights.astype(jnp.bfloat16))
        numer = jnp.einsum("hgqk,khd->qhgd", rounded.astype(jnp.float32), all_values.astype(jnp.float32))
        return (numer / jnp.transpose(total, (2, 0, 1))[..., None]).astype(jnp.bfloat16)

    result = lax.map(one_block, jnp.arange(N_SEQ, dtype=jnp.int32))
    return result.reshape(tokens_all, HQ * HEAD_SIZE)
```

```python
import math

import jax
import jax.numpy as jnp
from jax import lax
from jax.experimental import pallas as pl
from jax.experimental.pallas import tpu as pltpu
from jax.sharding import PartitionSpec as P

HEAD_SIZE = 128
QUERY_PER_KV = 2

attn_scale = 168.0 ** (-0.5)
log2_scale = attn_scale * math.log2(math.e)
powers = (1, 2, 4, 8)
TILE = 256
NEG = -1e30
CONTRACT_LAST = (((1,), (1,)), ((), ()))


def attend(visible, queries, keys, values, distances):
    tokens = queries.shape[0]
    behind = len(keys) - 1
    tile = min(TILE, tokens)

    def kernel(visible_ref, q_ref, *refs):
        k_refs, v_refs = refs[: behind + 1], refs[behind + 1 : 2 * behind + 2]
        o_ref, peak_ref, total_ref, numer_ref = refs[2 * behind + 2 :]
        block = lax.axis_index("seq")

        def step(query, rows, slot, count, diagonal):
            scores = lax.dot_general(
                query, k_refs[slot][:count, :], CONTRACT_LAST, preferred_element_type=jnp.float32
            )
            if diagonal:
                row = lax.broadcasted_iota(jnp.int32, scores.shape, 0) + (count - tile)
                column = lax.broadcasted_iota(jnp.int32, scores.shape, 1)
                scores = jnp.where(column <= row, scores, NEG)
            peak = jnp.max(scores, axis=1, keepdims=True)
            if not diagonal:
                before = peak_ref[rows, :]
                peak = jnp.maximum(before, peak)
            weights = jnp.exp2((scores - peak) * log2_scale)
            total = jnp.sum(weights, axis=1, keepdims=True)
            numer = jnp.dot(
                weights.astype(jnp.bfloat16), v_refs[slot][:count, :], preferred_element_type=jnp.float32
            )
            if not diagonal:
                shrink = jnp.exp2((before - peak) * log2_scale)
                total = total + total_ref[rows, :] * shrink
                numer = numer + numer_ref[rows, :] * shrink
            peak_ref[rows, :] = peak
            total_ref[rows, :] = total
            numer_ref[rows, :] = numer

        for start in range(0, tokens, tile):
            rows = pl.ds(start, tile)
            query = q_ref[rows, :]
            step(query, rows, 0, start + tile, True)
            for slot in range(behind):
                seen = (visible_ref[0, powers.index(distances[slot])] != 0) & (block >= distances[slot])

                @pl.when(seen)
                def _():
                    step(query, rows, slot + 1, tokens, False)

            o_ref[rows, :] = (numer_ref[rows, :] / total_ref[rows, :]).astype(o_ref.dtype)

    vmem = pl.BlockSpec(memory_space=pltpu.VMEM)
    pairs = tokens * tokens * (behind + 1)
    return pl.pallas_call(
        kernel,
        out_shape=jax.ShapeDtypeStruct(queries.shape, queries.dtype),
        in_specs=[pl.BlockSpec(memory_space=pltpu.SMEM)] + [vmem] * (1 + 2 * (behind + 1)),
        out_specs=vmem,
        scratch_shapes=[
            pltpu.VMEM((tokens, 1), jnp.float32),
            pltpu.VMEM((tokens, 1), jnp.float32),
            pltpu.VMEM((tokens, HEAD_SIZE), jnp.float32),
        ],
        cost_estimate=pl.CostEstimate(
            flops=4 * pairs * HEAD_SIZE, transcendentals=pairs, bytes_accessed=2 * (2 + 2 * (behind + 1)) * tokens * HEAD_SIZE
        ),
        compiler_params=pltpu.CompilerParams(vmem_limit_bytes=32 << 20),
    )(visible, queries, *keys, *values)


def body(queries, keys, values, visible):
    heads = lax.axis_size("head")
    blocks = lax.axis_size("seq")
    share = queries.shape[0]
    tokens = share * heads

    def by_head(array):
        parts = array.reshape(share, heads, -1).transpose(1, 0, 2)
        return lax.all_to_all(parts, "head", split_axis=0, concat_axis=0, tiled=True).reshape(tokens, -1)

    def shift(array, pairs):
        return lax.ppermute(array, "seq", [p for p in pairs if 0 <= p[0] < blocks and 0 <= p[1] < blocks])

    key_own = by_head(keys)
    value_own = by_head(values)
    query_own = by_head(queries)
    distances = tuple(d for d in powers if d < blocks)

    def behind(array):
        got = []
        for d in distances:
            got.append(shift(array, [(i, i + d) for i in range(blocks)]))
        return got

    all_keys = [key_own] + behind(key_own)
    all_values = [value_own] + behind(value_own)
    outputs = []
    for member in range(QUERY_PER_KV):
        query = query_own[:, member * HEAD_SIZE : (member + 1) * HEAD_SIZE]
        out = attend(visible, query, all_keys, all_values, distances)
        out = lax.all_to_all(out.reshape(heads, share, HEAD_SIZE), "head", split_axis=0, concat_axis=0, tiled=True)
        outputs.append(out)
    return jnp.stack(outputs, axis=1).transpose(2, 0, 1, 3).reshape(share, -1)


def solution(mesh):
    return jax.shard_map(
        body,
        mesh=mesh,
        in_specs=(
            P(("seq", "head"), None),
            P(("seq", "head"), None),
            P(("seq", "head"), None),
            P("seq", None),
        ),
        out_specs=P(("seq", "head"), None),
        check_vma=False,
    )
```

```python
import math

import jax
import jax.numpy as jnp
from jax import lax
from jax.experimental import pallas as pl
from jax.experimental.pallas import tpu as pltpu
from jax.sharding import PartitionSpec as P

HEAD_SIZE = 128
QUERY_PER_KV = 2

attn_scale = 168.0 ** (-0.5)
log2_scale = attn_scale * math.log2(math.e)
powers = (1, 2, 4, 8)
NEG = -1e30
TILE = 256
CHUNK = 64
LANES = 128
CONTRACT_LAST = (((1,), (1,)), ((), ()))


def attend(visible, queries, members, slots, state, last):
    heads = lax.axis_size("head")
    tokens = queries.shape[0]
    share = tokens // heads
    tile = min(TILE, tokens)
    chunk = min(CHUNK, tile)
    begin = state is None
    n_state = 3

    def kernel(visible_ref, q_ref, *refs):
        refs = list(refs)
        take = lambda n: [refs.pop(0) for _ in range(n)]
        k_refs, v_refs = take(len(slots)), take(len(slots))
        if not begin:
            state_in = take(n_state)
        if last:
            (o_ref,) = take(1)
            state_out = state_in
        else:
            state_out = take(n_state)
        if begin:
            state_in = state_out
        score_refs, weight_refs = take(2), take(2)
        block = lax.axis_index("seq")
        place = lax.axis_index("head")
        seen = [
            None if d == 0 else (visible_ref[0, powers.index(d)] != 0) & (block >= d) for d, _, _ in slots
        ]

        def finish(base, numer, total):
            out = (numer / jnp.sum(total, axis=1, keepdims=True)).astype(o_ref.dtype)
            size = min(share, tile)
            for part in range(0, tile, size):
                start = base + part
                goes = lax.rem(lax.div(start, share) + heads - place, heads)
                inside = pl.ds(pl.multiple_of(lax.rem(start, share), size), size)
                o_ref[goes, inside, :] = out[part : part + size, :]

        def run(items, base):
            diagonal = base if isinstance(base, int) else None

            def score(i):
                member, slot, count, offset = items[i]
                columns = pl.ds(member * HEAD_SIZE, HEAD_SIZE)
                score_refs[i % 2][:, :count] = lax.dot_general(
                    q_ref[pl.ds(base + offset, tile), columns],
                    k_refs[slot][:count, :],
                    CONTRACT_LAST,
                    preferred_element_type=jnp.float32,
                )

            def soften(i):
                member, slot, count, offset = items[i]
                own = slots[slot][0] == 0
                fresh = begin and slot == 0
                for r in range(0, tile, chunk):
                    rows = pl.ds(base + offset + r, chunk)

                    def scores(j):
                        got = score_refs[i % 2][r : r + chunk, j : j + LANES]
                        if own and j + LANES > diagonal + r:
                            row = lax.broadcasted_iota(jnp.int32, got.shape, 0) + (diagonal + r - j)
                            column = lax.broadcasted_iota(jnp.int32, got.shape, 1)
                            got = jnp.where(column <= row, got, NEG)
                        return got

                    lanes = [j for j in range(0, count, LANES) if not (own and j >= diagonal + r + chunk)]
                    peak = scores(0)
                    for j in lanes[1:]:
                        peak = jnp.maximum(peak, scores(j))
                    peak = jnp.max(peak, axis=1, keepdims=True)
                    if not own:
                        peak = jnp.where(seen[slot], peak, NEG)
                    peak = jnp.broadcast_to(peak, (chunk, LANES))
                    if not fresh:
                        peak_ref, total_ref, numer_ref = (
                            state_in if slot == 0 else (peak_run, total_run, numer_run)
                        )
                        before = peak_ref[member, rows, :]
                        peak = jnp.maximum(before, peak)
                        shrink = jnp.exp2((before - peak) * log2_scale)
                    peak_run[member, rows, :] = peak
                    base_of = peak if own else jnp.where(seen[slot], peak, -NEG)
                    total = None
                    for j in range(0, count, LANES):
                        if j in lanes:
                            weights = jnp.exp2((scores(j) - base_of) * log2_scale)
                            total = weights if total is None else total + weights
                        else:
                            weights = jnp.zeros((chunk, LANES), jnp.float32)
                        weight_refs[i % 2][r : r + chunk, j : j + LANES] = weights.astype(jnp.bfloat16)
                    if not fresh:
                        total = total_ref[member, rows, :] * shrink + total
                        numer_run[member, rows, :] = numer_ref[member, rows, :] * shrink
                    total_run[member, rows, :] = total

            def mix(i):
                member, slot, count, offset = items[i]
                rows = pl.ds(base + offset, tile)
                numer = jnp.dot(
                    weight_refs[i % 2][:, :count], v_refs[slot][:count, :], preferred_element_type=jnp.float32
                )
                if not (begin and slot == 0):
                    numer = numer_run[member, rows, :] + numer
                if last and slot == len(slots) - 1:
                    finish(base + offset, numer, total_run[member, rows, :])
                else:
                    numer_run[member, rows, :] = numer

            score(0)
            for i in range(len(items)):
                if i + 1 < len(items):
                    score(i + 1)
                if i > 0 and items[i - 1][::3] == items[i][::3]:
                    mix(i - 1)
                    soften(i)
                else:
                    soften(i)
                    if i > 0:
                        mix(i - 1)
            mix(len(items) - 1)

        if last:
            peak_run, total_run, numer_run = take(3)
        else:
            peak_run, total_run, numer_run = state_out

        if slots[0][0] == 0:
            for start in range(0, tokens, tile):
                run([(m, 0, start + tile, 0) for m in members], start)
        else:

            group = 2 * tile if tokens % (2 * tile) == 0 else tile
            order = [
                (m, slot, tokens, offset)
                for slot in range(len(slots))
                for offset in range(0, group, tile)
                for m in members
            ]

            @pl.loop(0, tokens // group)
            def _(step):
                run(order, pl.multiple_of(step * group, group))

    vmem = pl.BlockSpec(memory_space=pltpu.VMEM)
    pairs = tokens * tokens * len(slots) * len(members)
    whole = jax.ShapeDtypeStruct((QUERY_PER_KV, tokens, LANES), jnp.float32)
    scratch = [pltpu.VMEM((tile, tokens), jnp.float32)] * 2 + [pltpu.VMEM((tile, tokens), jnp.bfloat16)] * 2
    if last:
        out_shape = jax.ShapeDtypeStruct((heads, share, HEAD_SIZE), queries.dtype)
        scratch += [pltpu.VMEM(whole.shape, jnp.float32)] * 3
    else:
        out_shape = [whole] * n_state
    operands = [visible, queries] + [k for _, k, _ in slots] + [v for _, _, v in slots] + list(state or ())
    aliases = {}
    if not begin and not last:
        aliases = {len(operands) - n_state + i: i for i in range(n_state)}
    return pl.pallas_call(
        kernel,
        out_shape=out_shape,
        in_specs=[pl.BlockSpec(memory_space=pltpu.SMEM)] + [vmem] * (len(operands) - 1),
        out_specs=vmem if last else [vmem] * n_state,
        scratch_shapes=scratch,
        input_output_aliases=aliases,
        cost_estimate=pl.CostEstimate(
            flops=4 * pairs * HEAD_SIZE, transcendentals=pairs, bytes_accessed=8 * tokens * HEAD_SIZE * len(slots)
        ),
        compiler_params=pltpu.CompilerParams(vmem_limit_bytes=14 << 20),
    )(*operands)


def split_by_head(arrays):
    heads = lax.axis_size("head")
    share = arrays[0].shape[0]
    widths = [array.shape[1] // heads for array in arrays]

    def kernel(*refs):
        place = lax.axis_index("head")
        sems = refs[-1]
        copies = []
        for i, width in enumerate(widths):
            for j in range(heads):
                start = pl.multiple_of(lax.rem(place + j, heads) * width, HEAD_SIZE)
                at = i * heads + j
                copies.append(
                    pltpu.make_async_copy(refs[i].at[:, pl.ds(start, width)], refs[len(widths) + at], sems.at[at])
                )
        for copy in copies:
            copy.start()
        for copy in copies:
            copy.wait()

    vmem = pl.BlockSpec(memory_space=pltpu.VMEM)
    pieces = pl.pallas_call(
        kernel,
        out_shape=[
            jax.ShapeDtypeStruct((share, width), arrays[0].dtype) for width in widths for _ in range(heads)
        ],
        in_specs=[pl.BlockSpec(memory_space=pltpu.HBM)] * len(widths),
        out_specs=[vmem] * (heads * len(widths)),
        scratch_shapes=[pltpu.SemaphoreType.DMA((heads * len(widths),))],
        compiler_params=pltpu.CompilerParams(vmem_limit_bytes=8 << 20),
    )(*arrays)
    return [pieces[i * heads : (i + 1) * heads] for i in range(len(widths))]


def join_heads(pieces):
    heads = lax.axis_size("head")
    share, width = pieces[0][0].shape

    def kernel(*refs):
        place = lax.axis_index("head")
        out_ref = refs[-1]
        ins = iter(refs)
        for member in range(len(pieces)):
            for j in range(heads):
                source = lax.rem(place + heads - j, heads)
                start = pl.multiple_of((source * len(pieces) + member) * width, HEAD_SIZE)
                out_ref[:, pl.ds(start, width)] = next(ins)[...]

    vmem = pl.BlockSpec(memory_space=pltpu.VMEM)
    flat = [piece for group in pieces for piece in group]
    return pl.pallas_call(
        kernel,
        out_shape=jax.ShapeDtypeStruct((share, heads * len(pieces) * width), flat[0].dtype),
        in_specs=[vmem] * len(flat),
        out_specs=vmem,
        compiler_params=pltpu.CompilerParams(vmem_limit_bytes=8 << 20),
    )(*flat)


def body(queries, keys, values, visible):
    heads = lax.axis_size("head")
    blocks = lax.axis_size("seq")
    place = lax.axis_index("head")
    block = lax.axis_index("seq")
    share = queries.shape[0]
    tokens = share * heads

    def rotate(piece, by):
        return lax.ppermute(piece, "head", [(i, (i + by) % heads) for i in range(heads)])

    def gather_tokens(pieces):
        got = [piece if j == 0 else rotate(piece, j) for j, piece in enumerate(pieces)]
        whole = jnp.zeros((tokens, pieces[0].shape[1]), pieces[0].dtype)
        for j in range(heads):
            source = lax.rem(place + heads - j, heads)
            whole = lax.dynamic_update_slice(whole, got[j], (source * share, 0))
        return whole

    def move(array, pairs):
        return lax.ppermute(array, "seq", [p for p in pairs if 0 <= min(p) and max(p) < blocks])

    distances = tuple(d for d in powers if d < blocks)
    relayed = [b for b in range(4, blocks - 2) if b & 3 == 1]

    def behind(own):
        far = {}
        for d in distances:
            if d > 2:
                far[d] = move(own, [(b - d, b) for b in range(d, blocks)])
        got = dict(far)
        if 2 in distances:
            got[2] = move(own, [(b - 2, b) for b in range(2, blocks) if b not in relayed])
            if relayed:
                through = move(far[4], [(b + 2, b) for b in relayed])
                is_relayed = (block >= 4) & (block < blocks - 2) & (block & 3 == 1)
                got[2] = jnp.where(is_relayed, through, got[2])
        if 1 in distances:
            if 2 in distances and blocks % 2 == 0:
                out = jnp.where(block % 2 == 0, own, got[2])
                got[1] = move(out, [(b, b ^ 1) for b in range(blocks)])
            else:
                got[1] = move(own, [(b - 1, b) for b in range(1, blocks)])
        return got

    (key_parts,) = split_by_head([keys])
    (value_parts, query_parts) = split_by_head([values, queries])
    key_own = gather_tokens(key_parts)
    key_behind = behind(key_own)
    value_own = gather_tokens(value_parts)
    value_behind = behind(value_own)
    query_own = gather_tokens(query_parts)
    members = list(range(QUERY_PER_KV))
    far = [(d, key_behind[d], value_behind[d]) for d in reversed(distances) if d > 2]
    near = [(d, key_behind[d], value_behind[d]) for d in reversed(distances) if d <= 2]
    state = attend(visible, query_own, members, [(0, key_own, value_own)], None, False)
    if far:
        state = attend(visible, query_own, members, far, state, False)
    pieces = []
    for member in members:
        out = attend(visible, query_own, [member], near, state, True)
        pieces.append([out[0]] + [rotate(out[j], j) for j in range(1, heads)])
    return join_heads(pieces)


def solution(mesh):
    return jax.shard_map(
        body,
        mesh=mesh,
        in_specs=(
            P(("seq", "head"), None),
            P(("seq", "head"), None),
            P(("seq", "head"), None),
            P("seq", None),
        ),
        out_specs=P(("seq", "head"), None),
        check_vma=False,
    )
```

```python
import math

import jax
import jax.numpy as jnp
from jax import lax
from jax.experimental import pallas as pl
from jax.experimental.pallas import tpu as pltpu
from jax.sharding import PartitionSpec as P

HEAD_SIZE = 128
QUERY_PER_KV = 2

attn_scale = 168.0 ** (-0.5)
log2_scale = attn_scale * math.log2(math.e)
powers = (1, 2, 4, 8)
NEG = -1e30
TILE = 256
CHUNK = 64
LANES = 128
CONTRACT_LAST = (((1,), (1,)), ((), ()))


def attend(visible, queries, members, slots, state, last, goes=None):
    heads = lax.axis_size("head")
    tokens = queries.shape[0]
    share = tokens // heads
    tile = min(TILE, tokens)
    chunk = min(CHUNK, tile)
    begin = state is None
    by_goal = goes is not None
    n_state = 3

    def kernel(visible_ref, q_ref, *refs):
        refs = list(refs)
        take = lambda n: [refs.pop(0) for _ in range(n)]
        k_refs, v_refs = take(len(slots)), take(len(slots))
        if not begin:
            state_in = take(n_state)
        if last:
            (o_ref,) = take(1)
            state_out = state_in
        else:
            state_out = take(n_state)
        if begin:
            state_in = state_out
        score_refs, weight_refs = take(2), take(2)
        block = lax.axis_index("seq")
        place = lax.axis_index("head")
        seen = [
            None if d == 0 else (visible_ref[0, powers.index(d)] != 0) & (block >= d) for d, _, _ in slots
        ]

        if by_goal:
            offsets = [
                pl.multiple_of(lax.rem(place + j, heads) * share + sub, tile)
                for j in goes
                for sub in range(0, share, tile)
            ]
        else:
            offsets = list(range(0, tokens, tile))

        def finish(number, base, numer, total):
            out = (numer / jnp.sum(total, axis=1, keepdims=True)).astype(o_ref.dtype)
            if by_goal:
                each = share // tile
                o_ref[number // each, pl.ds(number % each * tile, tile), :] = out
                return
            size = min(share, tile)
            for part in range(0, tile, size):
                start = base + part
                goal = lax.rem(start // share + heads - place, heads)
                o_ref[goal, pl.ds(start % share, size), :] = out[part : part + size, :]

        def run(items):
            at = lambda i: offsets[items[i][3]]

            def score(i):
                member, slot, count, _ = items[i]
                columns = pl.ds(member * HEAD_SIZE, HEAD_SIZE)
                score_refs[i % 2][:, :count] = lax.dot_general(
                    q_ref[pl.ds(at(i), tile), columns],
                    k_refs[slot][:count, :],
                    CONTRACT_LAST,
                    preferred_element_type=jnp.float32,
                )

            def soften(i):
                member, slot, count, _ = items[i]
                own = slots[slot][0] == 0
                fresh = begin and slot == 0
                diagonal = at(i)
                for r in range(0, tile, chunk):
                    rows = pl.ds(at(i) + r, chunk)

                    def scores(j):
                        got = score_refs[i % 2][r : r + chunk, j : j + LANES]
                        if own and j + LANES > diagonal + r:
                            row = lax.broadcasted_iota(jnp.int32, got.shape, 0) + (diagonal + r - j)
                            column = lax.broadcasted_iota(jnp.int32, got.shape, 1)
                            got = jnp.where(column <= row, got, NEG)
                        return got

                    lanes = [j for j in range(0, count, LANES) if not (own and j >= diagonal + r + chunk)]
                    peak = scores(0)
                    for j in lanes[1:]:
                        peak = jnp.maximum(peak, scores(j))
                    peak = jnp.max(peak, axis=1, keepdims=True)
                    if not own:
                        peak = jnp.where(seen[slot], peak, NEG)
                    peak = jnp.broadcast_to(peak, (chunk, LANES))
                    if not fresh:
                        peak_ref, total_ref, numer_ref = (
                            state_in if slot == 0 else (peak_run, total_run, numer_run)
                        )
                        before = peak_ref[member, rows, :]
                        peak = jnp.maximum(before, peak)
                        shrink = jnp.exp2((before - peak) * log2_scale)
                    peak_run[member, rows, :] = peak
                    base_of = peak if own else jnp.where(seen[slot], peak, -NEG)
                    total = None
                    for j in range(0, count, LANES):
                        if j in lanes:
                            weights = jnp.exp2((scores(j) - base_of) * log2_scale)
                            total = weights if total is None else total + weights
                        else:
                            weights = jnp.zeros((chunk, LANES), jnp.float32)
                        weight_refs[i % 2][r : r + chunk, j : j + LANES] = weights.astype(jnp.bfloat16)
                    if not fresh:
                        total = total_ref[member, rows, :] * shrink + total
                        numer_run[member, rows, :] = numer_ref[member, rows, :] * shrink
                    total_run[member, rows, :] = total

            def mix(i):
                member, slot, count, number = items[i]
                rows = pl.ds(at(i), tile)
                numer = jnp.dot(
                    weight_refs[i % 2][:, :count], v_refs[slot][:count, :], preferred_element_type=jnp.float32
                )
                if not (begin and slot == 0):
                    numer = numer_run[member, rows, :] + numer
                if last and slot == len(slots) - 1:
                    finish(number, at(i), numer, total_run[member, rows, :])
                else:
                    numer_run[member, rows, :] = numer

            score(0)
            for i in range(len(items)):
                if i + 1 < len(items):
                    score(i + 1)
                if i > 0 and items[i - 1][::3] == items[i][::3]:
                    mix(i - 1)
                    soften(i)
                else:
                    soften(i)
                    if i > 0:
                        mix(i - 1)
            mix(len(items) - 1)

        if last:
            peak_run, total_run, numer_run = take(3)
        else:
            peak_run, total_run, numer_run = state_out

        run(
            [
                (m, slot, tokens if slots[slot][0] else (number + 1) * tile, number)
                for slot in range(len(slots))
                for number in range(len(offsets))
                for m in members
            ]
        )

    vmem = pl.BlockSpec(memory_space=pltpu.VMEM)
    pairs = tokens * tokens * len(slots) * len(members)
    whole = jax.ShapeDtypeStruct((QUERY_PER_KV, tokens, LANES), jnp.float32)
    scratch = [pltpu.VMEM((tile, tokens), jnp.float32)] * 2 + [pltpu.VMEM((tile, tokens), jnp.bfloat16)] * 2
    if last:
        out_shape = jax.ShapeDtypeStruct((len(goes) if by_goal else heads, share, HEAD_SIZE), queries.dtype)
        scratch += [pltpu.VMEM(whole.shape, jnp.float32)] * 3
    else:
        out_shape = [whole] * n_state
    operands = [visible, queries] + [k for _, k, _ in slots] + [v for _, _, v in slots] + list(state or ())
    aliases = {}
    if not begin and not last:
        aliases = {len(operands) - n_state + i: i for i in range(n_state)}
    return pl.pallas_call(
        kernel,
        out_shape=out_shape,
        in_specs=[pl.BlockSpec(memory_space=pltpu.SMEM)] + [vmem] * (len(operands) - 1),
        out_specs=vmem if last else [vmem] * n_state,
        scratch_shapes=scratch,
        input_output_aliases=aliases,
        cost_estimate=pl.CostEstimate(
            flops=4 * pairs * HEAD_SIZE, transcendentals=pairs, bytes_accessed=8 * tokens * HEAD_SIZE * len(slots)
        ),
        compiler_params=pltpu.CompilerParams(vmem_limit_bytes=14 << 20),
    )(*operands)


def split_by_head(arrays):
    heads = lax.axis_size("head")
    share = arrays[0].shape[0]
    widths = [array.shape[1] // heads for array in arrays]

    def kernel(*refs):
        place = lax.axis_index("head")
        sems = refs[-1]
        copies = []
        for i, width in enumerate(widths):
            for j in range(heads):
                start = pl.multiple_of(lax.rem(place + j, heads) * width, HEAD_SIZE)
                at = i * heads + j
                copies.append(
                    pltpu.make_async_copy(refs[i].at[:, pl.ds(start, width)], refs[len(widths) + at], sems.at[at])
                )
        for copy in copies:
            copy.start()
        for copy in copies:
            copy.wait()

    vmem = pl.BlockSpec(memory_space=pltpu.VMEM)
    pieces = pl.pallas_call(
        kernel,
        out_shape=[
            jax.ShapeDtypeStruct((share, width), arrays[0].dtype) for width in widths for _ in range(heads)
        ],
        in_specs=[pl.BlockSpec(memory_space=pltpu.HBM)] * len(widths),
        out_specs=[vmem] * (heads * len(widths)),
        scratch_shapes=[pltpu.SemaphoreType.DMA((heads * len(widths),))],
        compiler_params=pltpu.CompilerParams(vmem_limit_bytes=8 << 20),
    )(*arrays)
    return [pieces[i * heads : (i + 1) * heads] for i in range(len(widths))]


def join_heads(pieces):
    heads = lax.axis_size("head")
    share, width = pieces[0][0].shape

    def kernel(*refs):
        place = lax.axis_index("head")
        out_ref = refs[-1]
        ins = iter(refs)
        for member in range(len(pieces)):
            for j in range(heads):
                source = lax.rem(place + heads - j, heads)
                start = pl.multiple_of((source * len(pieces) + member) * width, HEAD_SIZE)
                out_ref[:, pl.ds(start, width)] = next(ins)[...]

    vmem = pl.BlockSpec(memory_space=pltpu.VMEM)
    flat = [piece for group in pieces for piece in group]
    return pl.pallas_call(
        kernel,
        out_shape=jax.ShapeDtypeStruct((share, heads * len(pieces) * width), flat[0].dtype),
        in_specs=[vmem] * len(flat),
        out_specs=vmem,
        compiler_params=pltpu.CompilerParams(vmem_limit_bytes=8 << 20),
    )(*flat)


def body(queries, keys, values, visible):
    heads = lax.axis_size("head")
    blocks = lax.axis_size("seq")
    place = lax.axis_index("head")
    block = lax.axis_index("seq")
    share = queries.shape[0]
    tokens = share * heads

    def rotate(piece, by):
        return lax.ppermute(piece, "head", [(i, (i + by) % heads) for i in range(heads)])

    def gather_tokens(pieces):
        got = [piece if j == 0 else rotate(piece, j) for j, piece in enumerate(pieces)]
        whole = jnp.zeros((tokens, pieces[0].shape[1]), pieces[0].dtype)
        for j in range(heads):
            source = lax.rem(place + heads - j, heads)
            whole = lax.dynamic_update_slice(whole, got[j], (source * share, 0))
        return whole

    def move(array, pairs):
        return lax.ppermute(array, "seq", [p for p in pairs if 0 <= min(p) and max(p) < blocks])

    distances = tuple(d for d in powers if d < blocks)
    relayed = [b for b in range(4, blocks - 2) if b & 3 == 1]

    def behind(own):
        far = {}
        for d in distances:
            if d > 2:
                far[d] = move(own, [(b - d, b) for b in range(d, blocks)])
        got = dict(far)
        if 2 in distances:
            got[2] = move(own, [(b - 2, b) for b in range(2, blocks) if b not in relayed])
            if relayed:
                through = move(far[4], [(b + 2, b) for b in relayed])
                is_relayed = (block >= 4) & (block < blocks - 2) & (block & 3 == 1)
                got[2] = jnp.where(is_relayed, through, got[2])
        if 1 in distances:
            if 2 in distances and blocks % 2 == 0:
                out = jnp.where(block % 2 == 0, own, got[2])
                got[1] = move(out, [(b, b ^ 1) for b in range(blocks)])
            else:
                got[1] = move(own, [(b - 1, b) for b in range(1, blocks)])
        return got

    (key_parts,) = split_by_head([keys])
    (value_parts, query_parts) = split_by_head([values, queries])
    key_own = gather_tokens(key_parts)
    key_behind = behind(key_own)
    value_own = gather_tokens(value_parts)
    value_behind = behind(value_own)
    query_own = gather_tokens(query_parts)
    members = list(range(QUERY_PER_KV))
    far = [(d, key_behind[d], value_behind[d]) for d in reversed(distances) if d > 2]
    near = [(d, key_behind[d], value_behind[d]) for d in reversed(distances) if d <= 2]
    state = attend(visible, query_own, members, [(0, key_own, value_own)], None, False)
    if far:
        state = attend(visible, query_own, members, far, state, False)
    pieces = []
    tile = min(TILE, tokens)
    for member in members:
        groups = [None]
        if member == members[-1] and share % tile == 0 and heads > 2:
            cut = heads // 2 + 1
            groups = [list(range(1, cut)), list(range(cut, heads)) + [0]]
        got = {}
        for goes in groups:
            out = attend(visible, query_own, [member], near, state, True, goes)
            for i, j in enumerate(goes or range(heads)):
                got[j] = rotate(out[i], j) if j else out[i]
        pieces.append([got[j] for j in range(heads)])
    return join_heads(pieces)


def solution(mesh):
    return jax.shard_map(
        body,
        mesh=mesh,
        in_specs=(
            P(("seq", "head"), None),
            P(("seq", "head"), None),
            P(("seq", "head"), None),
            P("seq", None),
        ),
        out_specs=P(("seq", "head"), None),
        check_vma=False,
    )
```

```python
import math

import jax
import jax.numpy as jnp
from jax import lax
from jax.experimental import pallas as pl
from jax.experimental.pallas import tpu as pltpu
from jax.sharding import PartitionSpec as P

HEAD_SIZE = 128
QUERY_PER_KV = 2

attn_scale = 168.0 ** (-0.5)
log2_scale = attn_scale * math.log2(math.e)
powers = (1, 2, 4, 8)
NEG = -1e30
TILE = 256
CHUNK = 64
LANES = 128
CONTRACT_LAST = (((1,), (1,)), ((), ()))


def attend(visible, queries, members, slots, state, last, goes=None):
    heads = lax.axis_size("head")
    tokens = queries.shape[0]
    share = tokens // heads
    tile = min(TILE, tokens)
    chunk = min(CHUNK, tile)
    begin = state is None
    by_goal = goes is not None
    n_state = 3

    def kernel(visible_ref, q_ref, *refs):
        refs = list(refs)
        take = lambda n: [refs.pop(0) for _ in range(n)]
        k_refs, v_refs = take(len(slots)), take(len(slots))
        if not begin:
            state_in = take(n_state)
        if last:
            (o_ref,) = take(1)
            state_out = state_in
        else:
            state_out = take(n_state)
        if begin:
            state_in = state_out
        score_refs, weight_refs = take(2), take(2)
        block = lax.axis_index("seq")
        place = lax.axis_index("head")
        seen = [
            None if d == 0 else (visible_ref[0, powers.index(d)] != 0) & (block >= d) for d, _, _ in slots
        ]

        if by_goal:
            offsets = [
                pl.multiple_of(lax.rem(place + j, heads) * share + sub, tile)
                for j in goes
                for sub in range(0, share, tile)
            ]
        else:
            offsets = list(range(0, tokens, tile))

        def finish(member, number, base, numer, total):
            columns = pl.ds(members.index(member) * HEAD_SIZE, HEAD_SIZE)
            out = (numer / jnp.sum(total, axis=1, keepdims=True)).astype(o_ref.dtype)
            if by_goal:
                each = share // tile
                o_ref[number // each, pl.ds(number % each * tile, tile), columns] = out
                return
            size = min(share, tile)
            for part in range(0, tile, size):
                start = base + part
                goal = lax.rem(start // share + heads - place, heads)
                o_ref[goal, pl.ds(start % share, size), columns] = out[part : part + size, :]

        def run(items):
            at = lambda i: offsets[items[i][3]]

            def score(i):
                member, slot, count, _ = items[i]
                columns = pl.ds(member * HEAD_SIZE, HEAD_SIZE)
                score_refs[i % 2][:, :count] = lax.dot_general(
                    q_ref[pl.ds(at(i), tile), columns],
                    k_refs[slot][:count, :],
                    CONTRACT_LAST,
                    preferred_element_type=jnp.float32,
                )

            def soften(i):
                member, slot, count, _ = items[i]
                own = slots[slot][0] == 0
                fresh = begin and slot == 0
                diagonal = at(i)
                for r in range(0, tile, chunk):
                    rows = pl.ds(at(i) + r, chunk)

                    def scores(j):
                        got = score_refs[i % 2][r : r + chunk, j : j + LANES]
                        if own and j + LANES > diagonal + r:
                            row = lax.broadcasted_iota(jnp.int32, got.shape, 0) + (diagonal + r - j)
                            column = lax.broadcasted_iota(jnp.int32, got.shape, 1)
                            got = jnp.where(column <= row, got, NEG)
                        return got

                    lanes = [j for j in range(0, count, LANES) if not (own and j >= diagonal + r + chunk)]
                    peak = scores(0)
                    for j in lanes[1:]:
                        peak = jnp.maximum(peak, scores(j))
                    peak = jnp.max(peak, axis=1, keepdims=True)
                    if not own:
                        peak = jnp.where(seen[slot], peak, NEG)
                    peak = jnp.broadcast_to(peak, (chunk, LANES))
                    if not fresh:
                        peak_ref, total_ref, numer_ref = (
                            state_in if slot == 0 else (peak_run, total_run, numer_run)
                        )
                        before = peak_ref[member, rows, :]
                        peak = jnp.maximum(before, peak)
                        shrink = jnp.exp2((before - peak) * log2_scale)
                    peak_run[member, rows, :] = peak
                    base_of = peak if own else jnp.where(seen[slot], peak, -NEG)
                    total = None
                    for j in range(0, count, LANES):
                        if j in lanes:
                            weights = jnp.exp2((scores(j) - base_of) * log2_scale)
                            total = weights if total is None else total + weights
                        else:
                            weights = jnp.zeros((chunk, LANES), jnp.float32)
                        weight_refs[i % 2][r : r + chunk, j : j + LANES] = weights.astype(jnp.bfloat16)
                    if not fresh:
                        total = total_ref[member, rows, :] * shrink + total
                        numer_run[member, rows, :] = numer_ref[member, rows, :] * shrink
                    total_run[member, rows, :] = total

            def mix(i):
                member, slot, count, number = items[i]
                rows = pl.ds(at(i), tile)
                numer = jnp.dot(
                    weight_refs[i % 2][:, :count], v_refs[slot][:count, :], preferred_element_type=jnp.float32
                )
                if not (begin and slot == 0):
                    numer = numer_run[member, rows, :] + numer
                if last and slot == len(slots) - 1:
                    finish(member, number, at(i), numer, total_run[member, rows, :])
                else:
                    numer_run[member, rows, :] = numer

            score(0)
            for i in range(len(items)):
                if i + 1 < len(items):
                    score(i + 1)
                if i > 0 and items[i - 1][::3] == items[i][::3]:
                    mix(i - 1)
                    soften(i)
                else:
                    soften(i)
                    if i > 0:
                        mix(i - 1)
            mix(len(items) - 1)

        if last:
            peak_run, total_run, numer_run = take(3)
        else:
            peak_run, total_run, numer_run = state_out

        run(
            [
                (m, slot, tokens if slots[slot][0] else (number + 1) * tile, number)
                for slot in range(len(slots))
                for number in range(len(offsets))
                for m in members
            ]
        )

    vmem = pl.BlockSpec(memory_space=pltpu.VMEM)
    pairs = tokens * tokens * len(slots) * len(members)
    whole = jax.ShapeDtypeStruct((QUERY_PER_KV, tokens, LANES), jnp.float32)
    scratch = [pltpu.VMEM((tile, tokens), jnp.float32)] * 2 + [pltpu.VMEM((tile, tokens), jnp.bfloat16)] * 2
    if last:
        out_shape = jax.ShapeDtypeStruct(
            (len(goes) if by_goal else heads, share, len(members) * HEAD_SIZE), queries.dtype
        )
        scratch += [pltpu.VMEM(whole.shape, jnp.float32)] * 3
    else:
        out_shape = [whole] * n_state
    operands = [visible, queries] + [k for _, k, _ in slots] + [v for _, _, v in slots] + list(state or ())
    aliases = {}
    if not begin and not last:
        aliases = {len(operands) - n_state + i: i for i in range(n_state)}
    return pl.pallas_call(
        kernel,
        out_shape=out_shape,
        in_specs=[pl.BlockSpec(memory_space=pltpu.SMEM)] + [vmem] * (len(operands) - 1),
        out_specs=vmem if last else [vmem] * n_state,
        scratch_shapes=scratch,
        input_output_aliases=aliases,
        cost_estimate=pl.CostEstimate(
            flops=4 * pairs * HEAD_SIZE, transcendentals=pairs, bytes_accessed=8 * tokens * HEAD_SIZE * len(slots)
        ),
        compiler_params=pltpu.CompilerParams(vmem_limit_bytes=14 << 20),
    )(*operands)


def split_by_head(arrays):
    heads = lax.axis_size("head")
    share = arrays[0].shape[0]
    widths = [array.shape[1] // heads for array in arrays]

    def kernel(*refs):
        place = lax.axis_index("head")
        sems = refs[-1]
        copies = []
        for i, width in enumerate(widths):
            for j in range(heads):
                start = pl.multiple_of(lax.rem(place + j, heads) * width, HEAD_SIZE)
                at = i * heads + j
                copies.append(
                    pltpu.make_async_copy(refs[i].at[:, pl.ds(start, width)], refs[len(widths) + at], sems.at[at])
                )
        for copy in copies:
            copy.start()
        for copy in copies:
            copy.wait()

    vmem = pl.BlockSpec(memory_space=pltpu.VMEM)
    pieces = pl.pallas_call(
        kernel,
        out_shape=[
            jax.ShapeDtypeStruct((share, width), arrays[0].dtype) for width in widths for _ in range(heads)
        ],
        in_specs=[pl.BlockSpec(memory_space=pltpu.HBM)] * len(widths),
        out_specs=[vmem] * (heads * len(widths)),
        scratch_shapes=[pltpu.SemaphoreType.DMA((heads * len(widths),))],
        compiler_params=pltpu.CompilerParams(vmem_limit_bytes=8 << 20),
    )(*arrays)
    return [pieces[i * heads : (i + 1) * heads] for i in range(len(widths))]


def join_heads(pieces):
    heads = lax.axis_size("head")
    share, width = pieces[0][0].shape

    def kernel(*refs):
        place = lax.axis_index("head")
        out_ref = refs[-1]
        ins = iter(refs)
        for member in range(len(pieces)):
            for j in range(heads):
                source = lax.rem(place + heads - j, heads)
                start = pl.multiple_of((source * len(pieces) + member) * width, HEAD_SIZE)
                out_ref[:, pl.ds(start, width)] = next(ins)[...]

    vmem = pl.BlockSpec(memory_space=pltpu.VMEM)
    flat = [piece for group in pieces for piece in group]
    return pl.pallas_call(
        kernel,
        out_shape=jax.ShapeDtypeStruct((share, heads * len(pieces) * width), flat[0].dtype),
        in_specs=[vmem] * len(flat),
        out_specs=vmem,
        compiler_params=pltpu.CompilerParams(vmem_limit_bytes=8 << 20),
    )(*flat)


def body(queries, keys, values, visible):
    heads = lax.axis_size("head")
    blocks = lax.axis_size("seq")
    place = lax.axis_index("head")
    block = lax.axis_index("seq")
    share = queries.shape[0]
    tokens = share * heads

    def rotate(piece, by):
        return lax.ppermute(piece, "head", [(i, (i + by) % heads) for i in range(heads)])

    def gather_tokens(pieces):
        got = {0: pieces[0]}
        for j in sorted(range(1, heads), key=lambda j: abs(2 * j - heads)):
            got[j] = rotate(pieces[j], j)
        whole = jnp.zeros((tokens, pieces[0].shape[1]), pieces[0].dtype)
        for j in range(heads):
            source = lax.rem(place + heads - j, heads)
            whole = lax.dynamic_update_slice(whole, got[j], (source * share, 0))
        return whole

    def move(array, pairs):
        return lax.ppermute(array, "seq", [p for p in pairs if 0 <= min(p) and max(p) < blocks])

    distances = tuple(d for d in powers if d < blocks)
    relayed = [b for b in range(4, blocks - 2) if b & 3 == 1]

    def behind(own):
        far = {}
        for d in distances:
            if d > 2:
                far[d] = move(own, [(b - d, b) for b in range(d, blocks)])
        got = dict(far)
        if 2 in distances:
            got[2] = move(own, [(b - 2, b) for b in range(2, blocks) if b not in relayed])
            if relayed:
                through = move(far[4], [(b + 2, b) for b in relayed])
                is_relayed = (block >= 4) & (block < blocks - 2) & (block & 3 == 1)
                got[2] = jnp.where(is_relayed, through, got[2])
        if 1 in distances:
            if 2 in distances and blocks % 2 == 0:
                out = jnp.where(block % 2 == 0, own, got[2])
                got[1] = move(out, [(b, b ^ 1) for b in range(blocks)])
            else:
                got[1] = move(own, [(b - 1, b) for b in range(1, blocks)])
        return got

    (key_parts,) = split_by_head([keys])
    (value_parts, query_parts) = split_by_head([values, queries])
    key_own = gather_tokens(key_parts)
    key_behind = behind(key_own)
    value_own = gather_tokens(value_parts)
    value_behind = behind(value_own)
    query_own = gather_tokens(query_parts)
    members = list(range(QUERY_PER_KV))
    far = [(d, key_behind[d], value_behind[d]) for d in reversed(distances) if d > 2]
    near = [(d, key_behind[d], value_behind[d]) for d in reversed(distances) if d <= 2]
    state = attend(visible, query_own, members, [(0, key_own, value_own)], None, False)
    if far:
        state = attend(visible, query_own, members, far, state, False)
    groups = [None]
    if share % min(TILE, tokens) == 0:
        groups = [[j] for j in sorted(range(1, heads), key=lambda j: abs(2 * j - heads))] + [[0]]
    got = {}
    for goes in groups:
        out = attend(visible, query_own, members, near, state, True, goes)
        for i, j in enumerate(goes or range(heads)):
            got[j] = rotate(out[i], j) if j else out[i]
    pieces = [[got[j] for j in range(heads)]]
    return join_heads(pieces)


def solution(mesh):
    return jax.shard_map(
        body,
        mesh=mesh,
        in_specs=(
            P(("seq", "head"), None),
            P(("seq", "head"), None),
            P(("seq", "head"), None),
            P("seq", None),
        ),
        out_specs=P(("seq", "head"), None),
        check_vma=False,
    )
```
